32 devices in a mesh: groups: 2 (over x), view: 16 (over z, y, core).
Axes of the slice: x: 2, y: 2, z: 4, core: 2. Of those that a mesh axis runs over, the one named last changes fastest.
Arguments:
- ref_features: bfloat16 [256, 32, 384], P(('groups', 'view')), parts along dimension 0, may hold values from -6 to 6
- source_tiles: bfloat16 [1024, 2, 32, 384], P(('groups', 'view')), parts along dimension 0, may hold values from -6 to 6
- pair_lists: int32 [32, 4, 4], P(('groups', 'view')), parts along dimension 0, may hold values from -1 to 511, as said below
- view_counts: int32 [32], P(('groups', 'view')), parts along dimension 0, may hold values from 3 to 4, as said below
- disparities: int32 [16, 4], P('groups'), parts along dimension 0, may hold values from -48 to 48
- conv_first: bfloat16 [3, 3, 8, 3, 32], replicated, may hold values from -0.21875 to 0.21875
- bias_first: float32 [8], replicated, may hold values from -3 to 3
- conv_second: bfloat16 [16, 3, 3, 3, 8], replicated, may hold values from -0.4375 to 0.4375
- bias_second: float32 [16], replicated, may hold values from -3 to 3
Outputs:
- cost_features: float32 [8, 64, 16, 192], P('groups', 'view'), parts along dimension 0
The draws below stay inside these ranges and needn't reach their ends.
There are 2 independent parts, one for each index of `groups`. The reference program is written for one: setup_inputs(seed, part) draws one part's arguments, and reference() takes and returns one part's arrays. A program takes and returns all parts, laid end to end along the dimension named above; an argument that names none is the same for every part. Nothing has to cross between parts.
Inputs may be any that keep to these rules, and one draw needn't show every extreme that they name: pair_lists[v, s, b] is the tile holding rows 2b and 2b + 1 of source s of strip v; it is -1 exactly when s >= view_counts[v]; tile t lies on device t // 32 of the view axis; no strip takes more than 2 tiles from one device, and some strip takes exactly 2 from some device. `view_counts`: some strip uses 3 sources and some uses 4.
All inputs are finite; a program needn't handle non-finite values.
Results may differ from the reference program's by a relative error of at most 0.0028.
Values may be sent and summed in bfloat16 or wider, within the bound.
A program may use at most 128 MiB of HBM per device.

```python
import jax
import jax.numpy as jnp
from jax import lax

C = 32
C1 = 8
C2 = 16
COLS = 384
ROWS = 8
PLANES = 8
SOURCES = 4
SHIFT = 48
TILES_DEV = 32
STRIPS = 16
TILES = 512
HEIGHT = 128
BLOCKS = 4
CAP = 2


def survey_pairs(key):
    base_key = jax.random.fold_in(key, 7331)
    key_count, key_pick, key_pop, key_rows = jax.random.split(base_key, 4)
    view_counts = jax.random.randint(key_count, (STRIPS,), 3, 5)
    full_strip = jax.random.randint(key_pick, (), 0, STRIPS)
    strip_ids = jnp.arange(STRIPS)
    view_counts = jnp.where(strip_ids == full_strip, 4, view_counts)
    view_counts = jnp.where(strip_ids == (full_strip + 1) % STRIPS, 3, view_counts)
    popular = jax.random.randint(key_pop, (STRIPS,), 0, 4) * (STRIPS // 2 + 1)
    requests = SOURCES * BLOCKS
    least_full = max(-((STRIPS - requests) // (CAP - 1)), 1)
    most_full = requests // CAP

    def one_strip(strip_key):
        key_jitter, key_shuffle, key_tile, key_twins = jax.random.split(strip_key, 4)
        jitter = jax.random.randint(key_jitter, (STRIPS,), 0, 2 * STRIPS)
        ranking = popular + jitter
        ranked = jnp.argsort(-ranking, stable=True)
        full_count = jax.random.randint(key_twins, (), least_full, most_full + 1)
        shuffled = jax.random.permutation(key_shuffle, requests)
        owner_slot = jnp.where(shuffled < CAP * full_count, shuffled // CAP, shuffled - CAP * full_count + full_count)
        owners = ranked[owner_slot]
        local_ids = jax.random.randint(key_tile, (requests,), 0, TILES_DEV)
        return owners * TILES_DEV + local_ids
    tile_ids = jax.vmap(one_strip)(jax.random.split(key_rows, STRIPS)).reshape(STRIPS, SOURCES, BLOCKS)
    source_ids = jnp.arange(SOURCES)
    in_use = source_ids[None, :, None] < view_counts[:, None, None]
    pair_ids = jnp.where(in_use, tile_ids, -1)
    return (pair_ids.astype(jnp.int32), view_counts.astype(jnp.int32))


def draw_pair_lists(key, part):
    return survey_pairs(key)[0]


def draw_view_counts(key, part):
    return survey_pairs(key)[1]


def touch_ends(result, own_key, low, top_value):
    extent = result.shape
    spot = [jax.random.randint(jax.random.fold_in(own_key, axis), (), 0, extent[axis]) for axis in range(len(extent))]
    result = result.at[tuple(spot)].set(low)
    longest = extent.index(max(extent))
    spot[longest] = (spot[longest] + 1) % extent[longest]
    return result.at[tuple(spot)].set(top_value)


def block_scale(own_key, extent, cuts, low, largest):
    loudness, own = 1.0, jax.random.fold_in(own_key, 6)
    for axis_at, blocks in cuts:
        draws = jnp.exp(jax.random.uniform(jax.random.fold_in(own, axis_at), (blocks,), jnp.float32, low / len(cuts), largest / len(cuts)))
        loudness = loudness * jnp.repeat(draws, extent[axis_at] // blocks).reshape([-1 if axis == axis_at else 1 for axis in range(len(extent))])
    return loudness


def bell_draw(stream_key, shape, width, bound, pieces=(), held_as=jnp.bfloat16):
    values = width * jax.random.normal(stream_key, shape, jnp.float32)
    if pieces:
        values = values * block_scale(stream_key, shape, pieces, -0.22, 0.18)
    return jnp.clip(values, -bound, bound).astype(held_as)


def setup_inputs(seed: int = 0, part: int = 0) -> dict:
    splits = jax.random.split(jax.random.key(seed), 10)
    part_splits = jax.random.split(jax.random.fold_in(splits[9], part), 10)
    return {
        "ref_features": bell_draw(part_splits[0], (HEIGHT, C, COLS), 1.0, 6.0, ((0, 16),)),
        "source_tiles": bell_draw(part_splits[1], (TILES, 2, C, COLS), 1.0, 6.0, ((0, 16),)),
        "pair_lists": draw_pair_lists(jax.random.fold_in(jax.random.fold_in(splits[9], part), 71), part),
        "view_counts": draw_view_counts(jax.random.fold_in(jax.random.fold_in(splits[9], part), 71), part),
        "disparities": touch_ends(jax.random.randint(part_splits[4], (PLANES, SOURCES), 0 - SHIFT, SHIFT + 1), jax.random.fold_in(part_splits[4], 1), 0 - SHIFT, SHIFT).astype(jnp.int32),
        "conv_first": bell_draw(splits[5], (3, 3, C1, 3, C), (27 * C) ** -0.5, 0.21875),
        "bias_first": bell_draw(splits[6], (C1,), 0.5, 3.0, (), jnp.float32),
        "conv_second": bell_draw(splits[7], (C2, 3, 3, 3, C1), (27 * C1) ** -0.5, 0.4375),
        "bias_second": bell_draw(splits[8], (C2,), 0.5, 3.0, (), jnp.float32),
    }


def shifted(rows, offset):
    padded = jnp.pad(rows, ((0, 0), (0, 0), (SHIFT, SHIFT)))
    return lax.dynamic_slice_in_dim(padded, (SHIFT - offset).astype(jnp.int32), COLS, 2)


def strip_variance(ref_rows, pair_row, live_count, source_tiles, disparities):
    ref_wide = ref_rows.astype(jnp.float32)
    summed = jnp.broadcast_to(ref_wide, (PLANES,) + ref_wide.shape)
    squares = summed * summed
    for source in range(SOURCES):
        picked = source_tiles[jnp.maximum(pair_row[source], 0)].reshape(ROWS, C, COLS)
        warped = jax.vmap(lambda offset: shifted(picked, offset))(disparities[:, source]).astype(jnp.float32)
        weight = (source < live_count).astype(jnp.float32)
        summed = summed + weight * warped
        squares = squares + weight * warped * warped
    view_total = live_count.astype(jnp.float32) + 1.0
    view_mean = summed / view_total
    return (squares / view_total - view_mean * view_mean).astype(jnp.bfloat16)


def reference(ref_features, source_tiles, pair_lists, view_counts, disparities, conv_first, bias_first, conv_second, bias_second):
    strips = ref_features.reshape(STRIPS, ROWS, C, COLS)
    volume = lax.map(lambda packed: strip_variance(packed[0], packed[1], packed[2], source_tiles, disparities), (strips, pair_lists, view_counts))
    volume_wide = jnp.transpose(volume, (3, 1, 0, 2, 4)).reshape(1, C, PLANES, HEIGHT, COLS).astype(jnp.float32)
    kernel_one = jnp.transpose(conv_first, (2, 4, 0, 1, 3)).astype(jnp.float32)
    first_out = lax.conv_general_dilated(volume_wide, kernel_one, (1, 1, 1), ((1, 1), (1, 1), (1, 1)), dimension_numbers=("NCDHW", "OIDHW", "NCDHW"), precision=lax.Precision.HIGHEST)
    cost_first = jnp.maximum(first_out + bias_first[None, :, None, None, None], 0.0).astype(jnp.bfloat16)
    kernel_two = jnp.transpose(conv_second, (0, 4, 1, 2, 3)).astype(jnp.float32)
    second = lax.conv_general_dilated(cost_first.astype(jnp.float32), kernel_two, (2, 2, 2), ((1, 1), (1, 1), (1, 1)), dimension_numbers=("NCDHW", "OIDHW", "NCDHW"), precision=lax.Precision.HIGHEST)
    second = second + bias_second[None, :, None, None, None]
    return jnp.transpose(second[0], (1, 2, 0, 3))
```

```python
import jax
import jax.numpy as jnp
from jax import lax
from jax.experimental import pallas as pl
from jax.experimental.pallas import tpu as pltpu
from jax.sharding import PartitionSpec as P


def passed_along(x, axis, by):
    count = lax.axis_size(axis)
    pairs = [(i, i + by) for i in range(count) if 0 <= i + by < count]
    return lax.ppermute(x, axis, pairs)


def request_slots(flat_ids, slot_cap, tiles_dev):
    is_live = flat_ids >= 0
    owners = jnp.where(is_live, flat_ids // tiles_dev, -1)
    count_req = flat_ids.shape[0]
    earlier = jnp.arange(count_req)[None, :] < jnp.arange(count_req)[:, None]
    same_owner = (owners[:, None] == owners[None, :]) & earlier & is_live[None, :]
    slot_rank = jnp.sum(same_owner.astype(jnp.int32), axis=1)
    slot_ids = jnp.where(is_live, owners * slot_cap + slot_rank, -1)
    return (slot_ids, flat_ids % tiles_dev)


def request_table(slot_ids, local_ids, n_view, slot_cap):
    positions = jnp.arange(n_view * slot_cap)
    matches = slot_ids[:, None] == positions[None, :]
    wanted = jnp.sum(jnp.where(matches, local_ids[:, None] + 1, 0), axis=0) - 1
    return wanted.reshape(n_view, slot_cap)


def variance_kernel(slot_ref, disp_ref, count_ref, arrived_ref, ref_ref, out_ref, wide_ref):
    sources, blocks = slot_ref.shape
    planes = disp_ref.shape[0]
    tile_rows, n_cols = arrived_ref.shape[1:]
    live = count_ref[0]
    for source in range(sources):
        for block in range(blocks):
            slot = jnp.maximum(slot_ref[source, block], 0)
            tile = arrived_ref[slot].astype(jnp.float32)
            wide_ref[source, block * tile_rows : (block + 1) * tile_rows] = jnp.where(
                source < live, tile, 0.0
            )
    total = live.astype(jnp.float32) + 1.0
    inverse = 1.0 / jnp.full((1, n_cols), total, jnp.float32)
    chunk = 32
    column = lax.broadcasted_iota(jnp.int32, (chunk, n_cols), 1)

    def one_plane(plane, carry):
        offsets = [disp_ref[plane, source] for source in range(sources)]
        for row in range(ref_ref.shape[0] // chunk):
            at = slice(row * chunk, (row + 1) * chunk)
            summed = ref_ref[at].astype(jnp.float32)
            squares = summed * summed
            for source in range(sources):
                offset = offsets[source]
                turned = pltpu.roll(
                    wide_ref[source, at], jnp.where(offset < 0, offset + n_cols, offset), 1
                )
                origin = column - offset
                inside = (origin >= 0) & (origin < n_cols)
                turned = jnp.where(inside, turned, 0.0)
                summed = summed + turned
                squares = squares + turned * turned
            mean = summed * inverse
            out_ref[plane, at] = (squares * inverse - mean * mean).astype(jnp.bfloat16)
        return carry

    lax.fori_loop(0, planes, one_plane, 0)


def conv_kernel(
    first_strip_ref, var_ref, above_ref, below_ref, w1_ref, b1_ref, w2_ref, b2_ref, pick_ref,
    out_ref, acc_ref, cost_ref,
):
    planes, _, n_cols = var_ref.shape
    part = w1_ref.shape[0] // 9
    half_p, half_r, c2, half_x = out_ref.shape
    wide = pick_ref.shape[1] // 3
    weights = w1_ref[...]

    def one_plane(plane):
        block = jnp.concatenate([above_ref[plane], var_ref[plane], below_ref[plane]], axis=0)
        product = jnp.dot(weights, block, preferred_element_type=jnp.float32)
        for tap in range(3):
            target = plane + 1 - tap
            if 0 <= target < planes:
                piece = product[tap * 3 * part : (tap + 1) * 3 * part]
                if tap == 0 or (tap == 1 and plane == 0):
                    acc_ref[target] = piece
                else:
                    acc_ref[target] += piece

    column = lax.broadcasted_iota(jnp.int32, (part, n_cols), 1)
    row = lax.broadcasted_iota(jnp.int32, (part, n_cols), 0)
    hidden = (row < part // (var_ref.shape[1] // 32 + 2)) & (first_strip_ref[0] == 1)
    cost_ref[0] = jnp.zeros(cost_ref.shape[1:], cost_ref.dtype)

    def finish(plane):
        left = jnp.where(column == 0, 0.0, pltpu.roll(acc_ref[plane, 0:part], 1, 1))
        right = jnp.where(
            column == n_cols - 1, 0.0, pltpu.roll(acc_ref[plane, 2 * part : 3 * part], n_cols - 1, 1)
        )
        total = acc_ref[plane, part : 2 * part] + left + right + b1_ref[...]
        cost = jnp.where(hidden, 0.0, jnp.maximum(total, 0.0)).astype(jnp.bfloat16)
        spread = jnp.dot(cost, pick_ref[...], preferred_element_type=jnp.float32)
        spread = spread.astype(jnp.bfloat16)
        for tap in range(3):
            cost_ref[plane + 1, tap * part : (tap + 1) * part] = spread[
                :, tap * wide : (tap + 1) * wide
            ]

    def second(q):
        block = cost_ref[2 * q : 2 * q + 3].reshape(9 * part, wide)
        result = jnp.dot(w2_ref[...], block, preferred_element_type=jnp.float32)
        result = result + b2_ref[...]
        out_ref[q] = result[:, :half_x].reshape(half_r, c2, half_x)

    for plane in range(planes):
        one_plane(plane)
        if plane >= 1:
            finish(plane - 1)
            if plane % 2 == 0:
                second(plane // 2 - 1)
    finish(planes - 1)
    second(half_p - 1)


def banded_first(conv_first, rows_n):
    taps_p, taps_r, c1, taps_x, channels = conv_first.shape
    moved = jnp.transpose(conv_first, (0, 3, 2, 1, 4))
    bands = [
        jnp.pad(moved, ((0, 0), (0, 0), (0, 0), (hi, rows_n - hi), (0, 0))).reshape(
            taps_p, taps_x, c1, (rows_n + 3) * channels
        )
        for hi in range(rows_n + 1)
    ]
    bands.append(jnp.zeros_like(bands[0]))
    return jnp.stack(bands, axis=2).reshape(-1, (rows_n + 3) * channels)


def banded_second(conv_second, rows_n):
    c2, taps_p, taps_r, taps_x, c1 = conv_second.shape
    moved = jnp.transpose(conv_second, (0, 1, 3, 2, 4))
    bands = [
        jnp.pad(
            moved, ((0, 0), (0, 0), (0, 0), (2 * g, rows_n + 2 - taps_r - 2 * g), (0, 0))
        ).reshape(c2, -1)
        for g in range(rows_n // 2)
    ]
    return jnp.concatenate(bands, axis=0)


def on_device(
    ref_features,
    source_tiles,
    pair_lists,
    view_counts,
    disparities,
    conv_first,
    bias_first,
    conv_second,
    bias_second,
):
    n_view = lax.axis_size("view")
    rows_n, channels, n_cols = ref_features.shape
    tiles_dev = source_tiles.shape[0]
    _, sources, blocks = pair_lists.shape
    planes = disparities.shape[0]
    c1 = conv_first.shape[2]
    c2 = conv_second.shape[0]
    request_total = sources * blocks
    slot_cap = max(2, (request_total + n_view - 1) // n_view)
    flat_ids = pair_lists.reshape(request_total)
    slot_ids, local_ids = request_slots(flat_ids, slot_cap, tiles_dev)
    wanted = request_table(slot_ids, local_ids, n_view, slot_cap)
    outgoing = source_tiles[
        jnp.maximum(lax.all_to_all(wanted, "view", split_axis=0, concat_axis=0, tiled=True), 0)
    ]
    arrived = lax.all_to_all(outgoing, "view", split_axis=0, concat_axis=0, tiled=True)
    arrived = arrived.reshape(n_view * slot_cap, 2 * channels, n_cols)
    smem = pl.BlockSpec(memory_space=pltpu.SMEM)
    vmem = pl.BlockSpec(memory_space=pltpu.VMEM)
    volume = pl.pallas_call(
        variance_kernel,
        out_shape=jax.ShapeDtypeStruct((planes, rows_n * channels, n_cols), jnp.bfloat16),
        in_specs=[smem, smem, smem, vmem, vmem],
        out_specs=vmem,
        scratch_shapes=[pltpu.VMEM((sources, rows_n * channels, n_cols), jnp.float32)],
        name="variance",
    )(
        slot_ids.reshape(sources, blocks),
        disparities,
        view_counts,
        arrived,
        ref_features.reshape(rows_n * channels, n_cols),
    )
    above = passed_along(volume[:, (rows_n - 2) * channels :], "view", 1)
    below = passed_along(volume[:, :channels], "view", -1)
    w1 = banded_first(conv_first, rows_n)
    w2 = banded_second(conv_second, rows_n)
    part = (rows_n + 2) * c1
    half_x = n_cols // 2
    wide = -(-half_x // 128) * 128
    b1 = jnp.broadcast_to(bias_first[None, :, None], (rows_n + 2, c1, 1)).reshape(part, 1)
    b2 = jnp.broadcast_to(bias_second[None, :, None], (rows_n // 2, c2, 1)).reshape(-1, 1)
    x_in = jnp.arange(n_cols)[:, None, None]
    x_out = 2 * jnp.arange(wide)[None, None, :] + jnp.arange(3)[None, :, None] - 1
    pick = ((x_in == x_out) & (jnp.arange(wide) < half_x)).astype(jnp.bfloat16)
    pick = pick.reshape(n_cols, 3 * wide)
    first_strip = (lax.axis_index("view") == 0).astype(jnp.int32).reshape(1)
    return pl.pallas_call(
        conv_kernel,
        out_shape=jax.ShapeDtypeStruct((planes // 2, rows_n // 2, c2, half_x), jnp.float32),
        in_specs=[smem] + [vmem] * 8,
        out_specs=vmem,
        scratch_shapes=[
            pltpu.VMEM((planes, 3 * part, n_cols), jnp.float32),
            pltpu.VMEM((planes + 1, 3 * part, wide), jnp.bfloat16),
        ],
        name="convolutions",
    )(first_strip, volume, above, below, w1, b1, w2, b2, pick)


def solution(mesh):
    return jax.shard_map(
        on_device,
        mesh=mesh,
        in_specs=(
            P(("groups", "view"), None, None),
            P(("groups", "view"), None, None, None),
            P(("groups", "view"), None, None),
            P(("groups", "view")),
            P("groups", None),
            P(),
            P(),
            P(),
            P(),
        ),
        out_specs=P("groups", "view", None, None),
        check_vma=False,
    )
```

```python
import functools

import jax
import jax.numpy as jnp
from jax import lax
from jax.experimental import pallas as pl
from jax.experimental.pallas import tpu as pltpu
from jax.sharding import PartitionSpec as P


def passed_along(x, axis, by):
    count = lax.axis_size(axis)
    pairs = [(i, i + by) for i in range(count) if 0 <= i + by < count]
    return lax.ppermute(x, axis, pairs)


def request_slots(flat_ids, slot_cap, tiles_dev):
    is_live = flat_ids >= 0
    owners = jnp.where(is_live, flat_ids // tiles_dev, -1)
    count_req = flat_ids.shape[0]
    earlier = jnp.arange(count_req)[None, :] < jnp.arange(count_req)[:, None]
    same_owner = (owners[:, None] == owners[None, :]) & earlier & is_live[None, :]
    slot_rank = jnp.sum(same_owner.astype(jnp.int32), axis=1)
    slot_ids = jnp.where(is_live, owners * slot_cap + slot_rank, -1)
    return (slot_ids, flat_ids % tiles_dev)


def request_table(slot_ids, local_ids, n_view, slot_cap):
    positions = jnp.arange(n_view * slot_cap)
    matches = slot_ids[:, None] == positions[None, :]
    wanted = jnp.sum(jnp.where(matches, local_ids[:, None] + 1, 0), axis=0) - 1
    return wanted.reshape(n_view, slot_cap)


def variance_kernel(rows, slot_ref, disp_ref, count_ref, arrived_ref, ref_ref, *refs):
    out_refs, wide_ref = refs[:-1], refs[-1]
    sources = slot_ref.shape[0]
    planes = disp_ref.shape[0]
    tile_rows, n_cols = arrived_ref.shape[1:]
    chunk = tile_rows // 2
    live = count_ref[0]
    flat_rows = [row for group in rows for row in group]
    for source in range(sources):
        for place, row in enumerate(flat_rows):
            slot = jnp.maximum(slot_ref[source, row // 2], 0)
            start = (row % 2) * chunk
            tile = arrived_ref[slot, start : start + chunk].astype(jnp.float32)
            wide_ref[source, place] = jnp.where(source < live, tile, 0.0)
    total = live.astype(jnp.float32) + 1.0
    inverse = 1.0 / jnp.full((1, n_cols), total, jnp.float32)
    column = lax.broadcasted_iota(jnp.int32, (chunk, n_cols), 1)

    def one_plane(plane, carry):
        offsets = [disp_ref[plane, source] for source in range(sources)]
        place = 0
        for group, out_ref in zip(rows, out_refs):
            for at, row in enumerate(group):
                summed = ref_ref[row * chunk : (row + 1) * chunk].astype(jnp.float32)
                squares = summed * summed
                for source in range(sources):
                    offset = offsets[source]
                    turned = pltpu.roll(
                        wide_ref[source, place], jnp.where(offset < 0, offset + n_cols, offset), 1
                    )
                    origin = column - offset
                    inside = (origin >= 0) & (origin < n_cols)
                    turned = jnp.where(inside, turned, 0.0)
                    summed = summed + turned
                    squares = squares + turned * turned
                mean = summed * inverse
                out_ref[plane, at * chunk : (at + 1) * chunk] = (
                    squares * inverse - mean * mean
                ).astype(jnp.bfloat16)
                place += 1
        return carry

    lax.fori_loop(0, planes, one_plane, 0)


def variance(rows, slots, disparities, view_counts, arrived, ref_flat):
    planes = disparities.shape[0]
    sources = slots.shape[0]
    chunk, n_cols = (arrived.shape[1] // 2, arrived.shape[2])
    smem = pl.BlockSpec(memory_space=pltpu.SMEM)
    vmem = pl.BlockSpec(memory_space=pltpu.VMEM)
    count = sum(len(group) for group in rows)
    values = planes * count * chunk * n_cols
    return pl.pallas_call(
        functools.partial(variance_kernel, rows),
        out_shape=[
            jax.ShapeDtypeStruct((planes, len(group) * chunk, n_cols), jnp.bfloat16)
            for group in rows
        ],
        in_specs=[smem, smem, smem, vmem, vmem],
        out_specs=[vmem] * len(rows),
        scratch_shapes=[pltpu.VMEM((sources, count, chunk, n_cols), jnp.float32)],
        cost_estimate=pl.CostEstimate(
            flops=values * 40, bytes_accessed=values * 4, transcendentals=0
        ),
        compiler_params=pltpu.CompilerParams(vmem_limit_bytes=12 << 20),
        name="variance%d" % count,
    )(slots, disparities, view_counts, arrived, ref_flat)


def prepare_kernel(conv_ref, w1_ref, pick_ref):
    groups, c1, n_lanes = conv_ref.shape
    rows_out = w1_ref.shape[0] // (groups * c1)
    width = w1_ref.shape[1]
    channels = width // (rows_out + 1)
    for group in range(groups):
        base = conv_ref[group].astype(jnp.float32)
        pieces = [
            pltpu.roll(base, hi * channels, 1) if hi else base for hi in range(rows_out - 1)
        ]
        pieces.append(jnp.zeros_like(base))
        band = jnp.concatenate(pieces, axis=0).astype(jnp.bfloat16)
        size = rows_out * c1
        w1_ref[group * size : (group + 1) * size] = band[:, :width]
    n_cols = pick_ref.shape[0]
    wide = pick_ref.shape[1] // 3
    source = lax.broadcasted_iota(jnp.int32, (n_cols, wide), 0)
    target = lax.broadcasted_iota(jnp.int32, (n_cols, wide), 1)
    for tap in range(3):
        hit = (source == 2 * target + (tap - 1)) & (target < n_cols // 2)
        pick_ref[:, tap * wide : (tap + 1) * wide] = jnp.where(hit, 1.0, 0.0).astype(jnp.bfloat16)


def conv_kernel(
    first_strip_ref, above_ref, top_ref, mid_ref, low_ref, below_ref, w1_ref, b1_ref, w2_ref, b2_ref, pick_ref,
    out_ref, acc_ref, cost_ref,
):
    planes, _, n_cols = mid_ref.shape
    part = w1_ref.shape[0] // 9
    half_p, half_r, c2, half_x = out_ref.shape
    wide = pick_ref.shape[1] // 3
    weights = w1_ref[...]

    def one_plane(plane):
        strips = (above_ref, top_ref, mid_ref, low_ref, below_ref)
        block = jnp.concatenate([strip[plane] for strip in strips], axis=0)
        product = jnp.dot(weights, block, preferred_element_type=jnp.float32)
        for tap in range(3):
            target = plane + 1 - tap
            if 0 <= target < planes:
                piece = product[tap * 3 * part : (tap + 1) * 3 * part]
                if tap == 0 or (tap == 1 and plane == 0):
                    acc_ref[target] = piece
                else:
                    acc_ref[target] += piece

    column = lax.broadcasted_iota(jnp.int32, (part, n_cols), 1)
    row = lax.broadcasted_iota(jnp.int32, (part, n_cols), 0)
    hidden = (row < part // (2 * half_r + 2)) & (first_strip_ref[0] == 1)
    cost_ref[0] = jnp.zeros(cost_ref.shape[1:], cost_ref.dtype)

    def finish(plane):
        left = jnp.where(column == 0, 0.0, pltpu.roll(acc_ref[plane, 0:part], 1, 1))
        right = jnp.where(
            column == n_cols - 1, 0.0, pltpu.roll(acc_ref[plane, 2 * part : 3 * part], n_cols - 1, 1)
        )
        total = acc_ref[plane, part : 2 * part] + left + right + b1_ref[...]
        cost = jnp.where(hidden, 0.0, jnp.maximum(total, 0.0)).astype(jnp.bfloat16)
        spread = jnp.dot(cost, pick_ref[...], preferred_element_type=jnp.float32)
        spread = spread.astype(jnp.bfloat16)
        for tap in range(3):
            cost_ref[plane + 1, tap * part : (tap + 1) * part] = spread[
                :, tap * wide : (tap + 1) * wide
            ]

    def second(q):
        block = cost_ref[2 * q : 2 * q + 3].reshape(9 * part, wide)
        result = jnp.dot(w2_ref[...], block, preferred_element_type=jnp.float32)
        result = result + b2_ref[...]
        out_ref[q] = result[:, :half_x].reshape(half_r, c2, half_x)

    for plane in range(planes):
        one_plane(plane)
        if plane >= 1:
            finish(plane - 1)
            if plane % 2 == 0:
                second(plane // 2 - 1)
    finish(planes - 1)
    second(half_p - 1)


def prepare(conv_first, rows_n, n_cols, wide):
    taps_p, taps_r, c1, taps_x, channels = conv_first.shape
    width = (rows_n + 3) * channels
    lanes = -(-width // 128) * 128
    groups = taps_p * taps_x
    moved = jnp.transpose(conv_first, (0, 3, 2, 1, 4)).reshape(groups, c1, taps_r * channels)
    moved = jnp.pad(moved, ((0, 0), (0, 0), (0, lanes - taps_r * channels)))
    vmem = pl.BlockSpec(memory_space=pltpu.VMEM)
    return pl.pallas_call(
        prepare_kernel,
        out_shape=[
            jax.ShapeDtypeStruct((groups * (rows_n + 2) * c1, width), jnp.bfloat16),
            jax.ShapeDtypeStruct((n_cols, 3 * wide), jnp.bfloat16),
        ],
        in_specs=[vmem],
        out_specs=[vmem] * 2,
        cost_estimate=pl.CostEstimate(flops=2000000, bytes_accessed=1200000, transcendentals=0),
        compiler_params=pltpu.CompilerParams(vmem_limit_bytes=8 << 20),
        name="prepare",
    )(moved)


def banded_second(conv_second, rows_n):
    c2, taps_p, taps_r, taps_x, c1 = conv_second.shape
    moved = jnp.transpose(conv_second, (0, 1, 3, 2, 4))
    bands = [
        jnp.pad(
            moved, ((0, 0), (0, 0), (0, 0), (2 * g, rows_n + 2 - taps_r - 2 * g), (0, 0))
        ).reshape(c2, -1)
        for g in range(rows_n // 2)
    ]
    return jnp.concatenate(bands, axis=0)


def on_device(
    ref_features,
    source_tiles,
    pair_lists,
    view_counts,
    disparities,
    conv_first,
    bias_first,
    conv_second,
    bias_second,
):
    n_view = lax.axis_size("view")
    rows_n, channels, n_cols = ref_features.shape
    tiles_dev = source_tiles.shape[0]
    _, sources, blocks = pair_lists.shape
    planes = disparities.shape[0]
    c1 = conv_first.shape[2]
    c2 = conv_second.shape[0]
    request_total = sources * blocks
    slot_cap = max(2, (request_total + n_view - 1) // n_view)
    flat_ids = pair_lists.reshape(request_total)
    slot_ids, local_ids = request_slots(flat_ids, slot_cap, tiles_dev)
    wanted = request_table(slot_ids, local_ids, n_view, slot_cap)
    asked = lax.all_to_all(wanted, "view", split_axis=0, concat_axis=0, tiled=True)
    outgoing = source_tiles[jnp.maximum(asked, 0)]
    arrived = lax.all_to_all(outgoing, "view", split_axis=0, concat_axis=0, tiled=True)
    arrived = arrived.reshape(n_view * slot_cap, 2 * channels, n_cols)
    w2 = banded_second(conv_second, rows_n)
    part = (rows_n + 2) * c1
    half_x = n_cols // 2
    wide = -(-half_x // 128) * 128
    b1 = jnp.broadcast_to(bias_first[None, :, None], (rows_n + 2, c1, 1)).reshape(part, 1)
    b2 = jnp.broadcast_to(bias_second[None, :, None], (rows_n // 2, c2, 1)).reshape(-1, 1)
    w1, pick = prepare(conv_first, rows_n, n_cols, wide)
    ready = (arrived, w1, w2, b1, b2, pick)
    arrived, w1, w2, b1, b2, pick = lax.optimization_barrier(ready)
    slots = slot_ids.reshape(sources, blocks)
    ref_flat = ref_features.reshape(rows_n * channels, n_cols)
    warp = functools.partial(variance, slots=slots, disparities=disparities)
    warp = functools.partial(warp, view_counts=view_counts, arrived=arrived, ref_flat=ref_flat)
    low, top = warp(((rows_n - 2, rows_n - 1), (0,)))
    above = passed_along(low, "view", 1)
    below = passed_along(top, "view", -1)
    (mid,) = warp((tuple(range(1, rows_n - 2)),))
    smem = pl.BlockSpec(memory_space=pltpu.SMEM)
    vmem = pl.BlockSpec(memory_space=pltpu.VMEM)
    first_strip = (lax.axis_index("view") == 0).astype(jnp.int32).reshape(1)
    return pl.pallas_call(
        conv_kernel,
        out_shape=jax.ShapeDtypeStruct((planes // 2, rows_n // 2, c2, half_x), jnp.float32),
        in_specs=[smem] + [vmem] * 10,
        out_specs=vmem,
        scratch_shapes=[
            pltpu.VMEM((planes, 3 * part, n_cols), jnp.float32),
            pltpu.VMEM((planes + 1, 3 * part, wide), jnp.bfloat16),
        ],
        compiler_params=pltpu.CompilerParams(vmem_limit_bytes=24 << 20),
        name="convolutions",
    )(first_strip, above, top, mid, low, below, w1, b1, w2, b2, pick)


def solution(mesh):
    return jax.shard_map(
        on_device,
        mesh=mesh,
        in_specs=(
            P(("groups", "view"), None, None),
            P(("groups", "view"), None, None, None),
            P(("groups", "view"), None, None),
            P(("groups", "view")),
            P("groups", None),
            P(),
            P(),
            P(),
            P(),
        ),
        out_specs=P("groups", "view", None, None),
        check_vma=False,
    )
```

```python
import functools

import jax
import jax.numpy as jnp
from jax import lax
from jax.experimental import pallas as pl
from jax.experimental.pallas import tpu as pltpu
from jax.sharding import PartitionSpec as P


def passed_along(x, axis, by):
    count = lax.axis_size(axis)
    pairs = [(i, i + by) for i in range(count) if 0 <= i + by < count]
    return lax.ppermute(x, axis, pairs)


def request_slots(flat_ids, slot_cap, tiles_dev):
    is_live = flat_ids >= 0
    owners = jnp.where(is_live, flat_ids // tiles_dev, -1)
    count_req = flat_ids.shape[0]
    earlier = jnp.arange(count_req)[None, :] < jnp.arange(count_req)[:, None]
    same_owner = (owners[:, None] == owners[None, :]) & earlier & is_live[None, :]
    slot_rank = jnp.sum(same_owner.astype(jnp.int32), axis=1)
    slot_ids = jnp.where(is_live, owners * slot_cap + slot_rank, -1)
    return (slot_ids, flat_ids % tiles_dev)


def request_table(slot_ids, local_ids, n_view, slot_cap):
    positions = jnp.arange(n_view * slot_cap)
    matches = slot_ids[:, None] == positions[None, :]
    wanted = jnp.sum(jnp.where(matches, local_ids[:, None] + 1, 0), axis=0) - 1
    return wanted.reshape(n_view, slot_cap)


def ask_kernel(n_view, wanted_ref, asked_ref, send_sem, recv_sem):
    me = lax.axis_index("view")
    mesh_id = pl.DeviceIdType.MESH
    barrier = pltpu.get_barrier_semaphore()

    def greet(step, carry):
        peer = lax.rem(me + step, n_view)
        pl.semaphore_signal(barrier, inc=1, device_id={"view": peer}, device_id_type=mesh_id)
        return carry

    lax.fori_loop(1, n_view, greet, 0)
    pl.semaphore_wait(barrier, n_view - 1)

    def ask(step, carry):
        peer = lax.rem(me + step, n_view)
        pltpu.make_async_remote_copy(
            src_ref=wanted_ref.at[peer],
            dst_ref=asked_ref.at[me],
            send_sem=send_sem.at[peer],
            recv_sem=recv_sem.at[me],
            device_id={"view": peer},
            device_id_type=mesh_id,
        ).start()
        return carry

    lax.fori_loop(1, n_view, ask, 0)
    asked_ref[me] = wanted_ref[me]

    def settle(step, carry):
        peer = lax.rem(me + step, n_view)
        copy = pltpu.make_async_remote_copy(
            src_ref=wanted_ref.at[peer],
            dst_ref=asked_ref.at[peer],
            send_sem=send_sem.at[peer],
            recv_sem=recv_sem.at[peer],
            device_id={"view": peer},
            device_id_type=mesh_id,
        )
        copy.wait_send()
        copy.wait_recv()
        return carry

    lax.fori_loop(1, n_view, settle, 0)


def ask_owners(wanted):
    n_view, slot_cap = wanted.shape
    table = jnp.broadcast_to(
        jnp.pad(wanted, ((0, 0), (0, 128 - slot_cap)))[:, None, :], (n_view, 8, 128)
    )
    vmem = pl.BlockSpec(memory_space=pltpu.VMEM)
    asked = pl.pallas_call(
        functools.partial(ask_kernel, n_view),
        out_shape=jax.ShapeDtypeStruct(table.shape, jnp.int32),
        in_specs=[vmem],
        out_specs=vmem,
        scratch_shapes=[pltpu.SemaphoreType.DMA((n_view,)), pltpu.SemaphoreType.DMA((n_view,))],
        compiler_params=pltpu.CompilerParams(
            collective_id=0, has_side_effects=True, vmem_limit_bytes=4 << 20
        ),
        name="ask",
    )(table)
    return asked[:, 0, :slot_cap]


def variance_kernel(rows, slot_ref, disp_ref, count_ref, arrived_ref, ref_ref, *refs):
    out_refs, wide_ref = refs[:-1], refs[-1]
    sources = slot_ref.shape[0]
    planes = disp_ref.shape[0]
    tile_rows, n_cols = arrived_ref.shape[1:]
    chunk = tile_rows // 2
    live = count_ref[0]
    flat_rows = [row for group in rows for row in group]
    for source in range(sources):
        for place, row in enumerate(flat_rows):
            slot = jnp.maximum(slot_ref[source, row // 2], 0)
            start = (row % 2) * chunk
            tile = arrived_ref[slot, start : start + chunk].astype(jnp.float32)
            wide_ref[source, place] = jnp.where(source < live, tile, 0.0)
    total = live.astype(jnp.float32) + 1.0
    inverse = 1.0 / jnp.full((1, n_cols), total, jnp.float32)
    column = lax.broadcasted_iota(jnp.int32, (chunk, n_cols), 1)

    def one_plane(plane, carry):
        offsets = [disp_ref[plane, source] for source in range(sources)]
        place = 0
        for group, out_ref in zip(rows, out_refs):
            for at, row in enumerate(group):
                summed = ref_ref[row * chunk : (row + 1) * chunk].astype(jnp.float32)
                squares = summed * summed
                for source in range(sources):
                    offset = offsets[source]
                    turned = pltpu.roll(
                        wide_ref[source, place], jnp.where(offset < 0, offset + n_cols, offset), 1
                    )
                    origin = column - offset
                    inside = (origin >= 0) & (origin < n_cols)
                    turned = jnp.where(inside, turned, 0.0)
                    summed = summed + turned
                    squares = squares + turned * turned
                mean = summed * inverse
                out_ref[plane, at * chunk : (at + 1) * chunk] = (
                    squares * inverse - mean * mean
                ).astype(jnp.bfloat16)
                place += 1
        return carry

    lax.fori_loop(0, planes, one_plane, 0)


def variance(rows, slots, disparities, view_counts, arrived, ref_flat):
    planes = disparities.shape[0]
    sources = slots.shape[0]
    chunk, n_cols = (arrived.shape[1] // 2, arrived.shape[2])
    smem = pl.BlockSpec(memory_space=pltpu.SMEM)
    vmem = pl.BlockSpec(memory_space=pltpu.VMEM)
    count = sum(len(group) for group in rows)
    values = planes * count * chunk * n_cols
    return pl.pallas_call(
        functools.partial(variance_kernel, rows),
        out_shape=[
            jax.ShapeDtypeStruct((planes, len(group) * chunk, n_cols), jnp.bfloat16)
            for group in rows
        ],
        in_specs=[smem, smem, smem, vmem, vmem],
        out_specs=[vmem] * len(rows),
        scratch_shapes=[pltpu.VMEM((sources, count, chunk, n_cols), jnp.float32)],
        cost_estimate=pl.CostEstimate(
            flops=values * 40, bytes_accessed=values * 4, transcendentals=0
        ),
        compiler_params=pltpu.CompilerParams(vmem_limit_bytes=12 << 20),
        name="variance%d" % count,
    )(slots, disparities, view_counts, arrived, ref_flat)


def prepare_kernel(conv_ref, w1_ref, pick_ref):
    groups, c1, n_lanes = conv_ref.shape
    rows_out = w1_ref.shape[0] // (groups * c1)
    width = w1_ref.shape[1]
    channels = width // (rows_out + 1)
    for group in range(groups):
        base = conv_ref[group].astype(jnp.float32)
        pieces = [
            pltpu.roll(base, hi * channels, 1) if hi else base for hi in range(rows_out - 1)
        ]
        pieces.append(jnp.zeros_like(base))
        band = jnp.concatenate(pieces, axis=0).astype(jnp.bfloat16)
        size = rows_out * c1
        w1_ref[group * size : (group + 1) * size] = band[:, :width]
    n_cols = pick_ref.shape[0]
    wide = pick_ref.shape[1] // 3
    source = lax.broadcasted_iota(jnp.int32, (n_cols, wide), 0)
    target = lax.broadcasted_iota(jnp.int32, (n_cols, wide), 1)
    for tap in range(3):
        hit = (source == 2 * target + (tap - 1)) & (target < n_cols // 2)
        pick_ref[:, tap * wide : (tap + 1) * wide] = jnp.where(hit, 1.0, 0.0).astype(jnp.bfloat16)


def conv_kernel(
    first_strip_ref, above_ref, top_ref, mid_ref, low_ref, below_ref, w1_ref, b1_ref, w2_ref, b2_ref, pick_ref,
    out_ref, acc_ref, cost_ref,
):
    planes, _, n_cols = mid_ref.shape
    part = w1_ref.shape[0] // 9
    half_p, half_r, c2, half_x = out_ref.shape
    wide = pick_ref.shape[1] // 3
    weights = w1_ref[...]

    def one_plane(plane):
        strips = (above_ref, top_ref, mid_ref, low_ref, below_ref)
        block = jnp.concatenate([strip[plane] for strip in strips], axis=0)
        product = jnp.dot(weights, block, preferred_element_type=jnp.float32)
        for tap in range(3):
            target = plane + 1 - tap
            if 0 <= target < planes:
                piece = product[tap * 3 * part : (tap + 1) * 3 * part]
                if tap == 0 or (tap == 1 and plane == 0):
                    acc_ref[target] = piece
                else:
                    acc_ref[target] += piece

    column = lax.broadcasted_iota(jnp.int32, (part, n_cols), 1)
    row = lax.broadcasted_iota(jnp.int32, (part, n_cols), 0)
    hidden = (row < part // (2 * half_r + 2)) & (first_strip_ref[0] == 1)
    cost_ref[0] = jnp.zeros(cost_ref.shape[1:], cost_ref.dtype)

    def finish(plane):
        left = jnp.where(column == 0, 0.0, pltpu.roll(acc_ref[plane, 0:part], 1, 1))
        right = jnp.where(
            column == n_cols - 1, 0.0, pltpu.roll(acc_ref[plane, 2 * part : 3 * part], n_cols - 1, 1)
        )
        total = acc_ref[plane, part : 2 * part] + left + right + b1_ref[...]
        cost = jnp.where(hidden, 0.0, jnp.maximum(total, 0.0)).astype(jnp.bfloat16)
        spread = jnp.dot(cost, pick_ref[...], preferred_element_type=jnp.float32)
        spread = spread.astype(jnp.bfloat16)
        for tap in range(3):
            cost_ref[plane + 1, tap * part : (tap + 1) * part] = spread[
                :, tap * wide : (tap + 1) * wide
            ]

    def second(q):
        block = cost_ref[2 * q : 2 * q + 3].reshape(9 * part, wide)
        result = jnp.dot(w2_ref[...], block, preferred_element_type=jnp.float32)
        result = result + b2_ref[...]
        out_ref[q] = result[:, :half_x].reshape(half_r, c2, half_x)

    for plane in range(planes):
        one_plane(plane)
        if plane >= 1:
            finish(plane - 1)
            if plane % 2 == 0:
                second(plane // 2 - 1)
    finish(planes - 1)
    second(half_p - 1)


def prepare(conv_first, rows_n, n_cols, wide):
    taps_p, taps_r, c1, taps_x, channels = conv_first.shape
    width = (rows_n + 3) * channels
    lanes = -(-width // 128) * 128
    groups = taps_p * taps_x
    moved = jnp.transpose(conv_first, (0, 3, 2, 1, 4)).reshape(groups, c1, taps_r * channels)
    moved = jnp.pad(moved, ((0, 0), (0, 0), (0, lanes - taps_r * channels)))
    vmem = pl.BlockSpec(memory_space=pltpu.VMEM)
    return pl.pallas_call(
        prepare_kernel,
        out_shape=[
            jax.ShapeDtypeStruct((groups * (rows_n + 2) * c1, width), jnp.bfloat16),
            jax.ShapeDtypeStruct((n_cols, 3 * wide), jnp.bfloat16),
        ],
        in_specs=[vmem],
        out_specs=[vmem] * 2,
        cost_estimate=pl.CostEstimate(flops=2000000, bytes_accessed=1200000, transcendentals=0),
        compiler_params=pltpu.CompilerParams(vmem_limit_bytes=8 << 20),
        name="prepare",
    )(moved)


def banded_second(conv_second, rows_n):
    c2, taps_p, taps_r, taps_x, c1 = conv_second.shape
    moved = jnp.transpose(conv_second, (0, 1, 3, 2, 4))
    bands = [
        jnp.pad(
            moved, ((0, 0), (0, 0), (0, 0), (2 * g, rows_n + 2 - taps_r - 2 * g), (0, 0))
        ).reshape(c2, -1)
        for g in range(rows_n // 2)
    ]
    return jnp.concatenate(bands, axis=0)


def on_device(
    ref_features,
    source_tiles,
    pair_lists,
    view_counts,
    disparities,
    conv_first,
    bias_first,
    conv_second,
    bias_second,
):
    n_view = lax.axis_size("view")
    rows_n, channels, n_cols = ref_features.shape
    tiles_dev = source_tiles.shape[0]
    _, sources, blocks = pair_lists.shape
    planes = disparities.shape[0]
    c1 = conv_first.shape[2]
    c2 = conv_second.shape[0]
    request_total = sources * blocks
    slot_cap = max(2, (request_total + n_view - 1) // n_view)
    flat_ids = pair_lists.reshape(request_total)
    slot_ids, local_ids = request_slots(flat_ids, slot_cap, tiles_dev)
    wanted = request_table(slot_ids, local_ids, n_view, slot_cap)
    asked = ask_owners(wanted)
    outgoing = source_tiles[jnp.maximum(asked, 0)]
    arrived = lax.all_to_all(outgoing, "view", split_axis=0, concat_axis=0, tiled=True)
    arrived = arrived.reshape(n_view * slot_cap, 2 * channels, n_cols)
    w2 = banded_second(conv_second, rows_n)
    part = (rows_n + 2) * c1
    half_x = n_cols // 2
    wide = -(-half_x // 128) * 128
    b1 = jnp.broadcast_to(bias_first[None, :, None], (rows_n + 2, c1, 1)).reshape(part, 1)
    b2 = jnp.broadcast_to(bias_second[None, :, None], (rows_n // 2, c2, 1)).reshape(-1, 1)
    w1, pick = prepare(conv_first, rows_n, n_cols, wide)
    ready = (arrived, w1, w2, b1, b2, pick)
    arrived, w1, w2, b1, b2, pick = lax.optimization_barrier(ready)
    slots = slot_ids.reshape(sources, blocks)
    ref_flat = ref_features.reshape(rows_n * channels, n_cols)
    warp = functools.partial(variance, slots=slots, disparities=disparities)
    warp = functools.partial(warp, view_counts=view_counts, arrived=arrived, ref_flat=ref_flat)
    low, top = warp(((rows_n - 2, rows_n - 1), (0,)))
    above = passed_along(low, "view", 1)
    below = passed_along(top, "view", -1)
    (mid,) = warp((tuple(range(1, rows_n - 2)),))
    smem = pl.BlockSpec(memory_space=pltpu.SMEM)
    vmem = pl.BlockSpec(memory_space=pltpu.VMEM)
    first_strip = (lax.axis_index("view") == 0).astype(jnp.int32).reshape(1)
    return pl.pallas_call(
        conv_kernel,
        out_shape=jax.ShapeDtypeStruct((planes // 2, rows_n // 2, c2, half_x), jnp.float32),
        in_specs=[smem] + [vmem] * 10,
        out_specs=vmem,
        scratch_shapes=[
            pltpu.VMEM((planes, 3 * part, n_cols), jnp.float32),
            pltpu.VMEM((planes + 1, 3 * part, wide), jnp.bfloat16),
        ],
        compiler_params=pltpu.CompilerParams(vmem_limit_bytes=24 << 20),
        name="convolutions",
    )(first_strip, above, top, mid, low, below, w1, b1, w2, b2, pick)


def solution(mesh):
    return jax.shard_map(
        on_device,
        mesh=mesh,
        in_specs=(
            P(("groups", "view"), None, None),
            P(("groups", "view"), None, None, None),
            P(("groups", "view"), None, None),
            P(("groups", "view")),
            P("groups", None),
            P(),
            P(),
            P(),
            P(),
        ),
        out_specs=P("groups", "view", None, None),
        check_vma=False,
    )
```

```python
import functools

import jax
import jax.numpy as jnp
from jax import lax
from jax.experimental import pallas as pl
from jax.experimental.pallas import tpu as pltpu
from jax.sharding import PartitionSpec as P


def passed_along(x, axis, by):
    count = lax.axis_size(axis)
    pairs = [(i, i + by) for i in range(count) if 0 <= i + by < count]
    return lax.ppermute(x, axis, pairs)


def request_slots(flat_ids, slot_cap, tiles_dev):
    is_live = flat_ids >= 0
    owners = jnp.where(is_live, flat_ids // tiles_dev, -1)
    count_req = flat_ids.shape[0]
    earlier = jnp.arange(count_req)[None, :] < jnp.arange(count_req)[:, None]
    same_owner = (owners[:, None] == owners[None, :]) & earlier & is_live[None, :]
    slot_rank = jnp.sum(same_owner.astype(jnp.int32), axis=1)
    slot_ids = jnp.where(is_live, owners * slot_cap + slot_rank, -1)
    return (slot_ids, flat_ids % tiles_dev)


def request_table(slot_ids, local_ids, n_view, slot_cap):
    positions = jnp.arange(n_view * slot_cap)
    matches = slot_ids[:, None] == positions[None, :]
    wanted = jnp.sum(jnp.where(matches, local_ids[:, None] + 1, 0), axis=0) - 1
    return wanted.reshape(n_view, slot_cap)


def ask_kernel(n_view, wanted_ref, asked_ref, send_sem, recv_sem):
    me = lax.axis_index("view")
    mesh_id = pl.DeviceIdType.MESH
    barrier = pltpu.get_barrier_semaphore()

    def greet(step, carry):
        peer = lax.rem(me + step, n_view)
        pl.semaphore_signal(barrier, inc=1, device_id={"view": peer}, device_id_type=mesh_id)
        return carry

    lax.fori_loop(1, n_view, greet, 0)
    pl.semaphore_wait(barrier, n_view - 1)

    def ask(step, carry):
        peer = lax.rem(me + step, n_view)
        pltpu.make_async_remote_copy(
            src_ref=wanted_ref.at[peer],
            dst_ref=asked_ref.at[me],
            send_sem=send_sem.at[peer],
            recv_sem=recv_sem.at[me],
            device_id={"view": peer},
            device_id_type=mesh_id,
        ).start()
        return carry

    lax.fori_loop(1, n_view, ask, 0)
    asked_ref[me] = wanted_ref[me]

    def settle(step, carry):
        peer = lax.rem(me + step, n_view)
        copy = pltpu.make_async_remote_copy(
            src_ref=wanted_ref.at[peer],
            dst_ref=asked_ref.at[peer],
            send_sem=send_sem.at[peer],
            recv_sem=recv_sem.at[peer],
            device_id={"view": peer},
            device_id_type=mesh_id,
        )
        copy.wait_send()
        copy.wait_recv()
        return carry

    lax.fori_loop(1, n_view, settle, 0)


def ask_owners(wanted):
    n_view, slot_cap = wanted.shape
    table = jnp.broadcast_to(
        jnp.pad(wanted, ((0, 0), (0, 128 - slot_cap)))[:, None, :], (n_view, 8, 128)
    )
    vmem = pl.BlockSpec(memory_space=pltpu.VMEM)
    asked = pl.pallas_call(
        functools.partial(ask_kernel, n_view),
        out_shape=jax.ShapeDtypeStruct(table.shape, jnp.int32),
        in_specs=[vmem],
        out_specs=vmem,
        scratch_shapes=[pltpu.SemaphoreType.DMA((n_view,)), pltpu.SemaphoreType.DMA((n_view,))],
        compiler_params=pltpu.CompilerParams(
            collective_id=0, has_side_effects=True, vmem_limit_bytes=4 << 20
        ),
        name="ask",
    )(table)
    return asked[:, 0, :slot_cap]


def variance_kernel(rows, slot_ref, disp_ref, count_ref, arrived_ref, ref_ref, *refs):
    out_refs, wide_ref = refs[:-1], refs[-1]
    sources = slot_ref.shape[0]
    planes = disp_ref.shape[0]
    tile_rows, n_cols = arrived_ref.shape[1:]
    chunk = tile_rows // 2
    live = count_ref[0]
    flat_rows = [row for group in rows for row in group]
    for source in range(sources):
        for place, row in enumerate(flat_rows):
            slot = jnp.maximum(slot_ref[source, row // 2], 0)
            start = (row % 2) * chunk
            tile = arrived_ref[slot, start : start + chunk].astype(jnp.float32)
            wide_ref[source, place] = jnp.where(source < live, tile, 0.0)
    total = live.astype(jnp.float32) + 1.0
    inverse = 1.0 / jnp.full((1, n_cols), total, jnp.float32)
    column = lax.broadcasted_iota(jnp.int32, (chunk, n_cols), 1)

    def one_plane(plane, carry):
        offsets = [disp_ref[plane, source] for source in range(sources)]
        place = 0
        for group, out_ref in zip(rows, out_refs):
            for at, row in enumerate(group):
                summed = ref_ref[row * chunk : (row + 1) * chunk].astype(jnp.float32)
                squares = summed * summed
                for source in range(sources):
                    offset = offsets[source]
                    turned = pltpu.roll(
                        wide_ref[source, place], jnp.where(offset < 0, offset + n_cols, offset), 1
                    )
                    origin = column - offset
                    inside = (origin >= 0) & (origin < n_cols)
                    turned = jnp.where(inside, turned, 0.0)
                    summed = summed + turned
                    squares = squares + turned * turned
                mean = summed * inverse
                out_ref[plane, at * chunk : (at + 1) * chunk] = (
                    squares * inverse - mean * mean
                ).astype(jnp.bfloat16)
                place += 1
        return carry

    lax.fori_loop(0, planes, one_plane, 0)


def variance(rows, slots, disparities, view_counts, arrived, ref_flat):
    planes = disparities.shape[0]
    sources = slots.shape[0]
    chunk, n_cols = (arrived.shape[1] // 2, arrived.shape[2])
    smem = pl.BlockSpec(memory_space=pltpu.SMEM)
    vmem = pl.BlockSpec(memory_space=pltpu.VMEM)
    count = sum(len(group) for group in rows)
    values = planes * count * chunk * n_cols
    return pl.pallas_call(
        functools.partial(variance_kernel, rows),
        out_shape=[
            jax.ShapeDtypeStruct((planes, len(group) * chunk, n_cols), jnp.bfloat16)
            for group in rows
        ],
        in_specs=[smem, smem, smem, vmem, vmem],
        out_specs=[vmem] * len(rows),
        scratch_shapes=[pltpu.VMEM((sources, count, chunk, n_cols), jnp.float32)],
        cost_estimate=pl.CostEstimate(
            flops=values * 40, bytes_accessed=values * 4, transcendentals=0
        ),
        compiler_params=pltpu.CompilerParams(vmem_limit_bytes=12 << 20),
        name="variance%d" % count,
    )(slots, disparities, view_counts, arrived, ref_flat)


def prepare_kernel(conv_ref, w1_ref, pick_ref):
    groups, c1, n_lanes = conv_ref.shape
    rows_out = w1_ref.shape[0] // (groups * c1)
    width = w1_ref.shape[1]
    channels = width // (rows_out + 2)
    bands = []
    for group in range(groups):
        base = conv_ref[group].astype(jnp.float32)
        for hi in range(rows_out):
            bands.append(pltpu.roll(base, hi * channels, 1) if hi else base)
    w1_ref[...] = jnp.concatenate(bands, axis=0).astype(jnp.bfloat16)[:, :width]
    n_cols = pick_ref.shape[0]
    wide = pick_ref.shape[1] // 3
    source = lax.broadcasted_iota(jnp.int32, (n_cols, wide), 0)
    target = lax.broadcasted_iota(jnp.int32, (n_cols, wide), 1)
    for tap in range(3):
        hit = (source == 2 * target + (tap - 1)) & (target < n_cols // 2)
        pick_ref[:, tap * wide : (tap + 1) * wide] = jnp.where(hit, 1.0, 0.0).astype(jnp.bfloat16)


def conv_kernel(
    first_strip_ref, above_ref, top_ref, mid_ref, low_ref, below_ref, w1_ref, b1_ref, w2_ref, b2_ref, pick_ref,
    out_ref, acc_ref, cost_ref,
):
    planes, _, n_cols = mid_ref.shape
    half = w1_ref.shape[0] // 9
    part = 2 * half
    depth = w1_ref.shape[1]
    half_p, half_r, c2, half_x = out_ref.shape
    wide = pick_ref.shape[1] // 3
    weights = w1_ref[...]

    def one_plane(plane):
        strips = (above_ref, top_ref, mid_ref, low_ref, below_ref)
        block = jnp.concatenate([strip[plane] for strip in strips], axis=0)
        skip = depth // (half_r + 3) * (half_r + 1)
        lower = block[skip:]
        products = (
            jnp.dot(weights, block[:depth], preferred_element_type=jnp.float32),
            jnp.dot(weights[:, : lower.shape[0]], lower, preferred_element_type=jnp.float32),
        )
        for tap in range(3):
            target = plane + 1 - tap
            if 0 <= target < planes:
                for shift in range(3):
                    for side in range(2):
                        start = (tap * 3 + shift) * half
                        piece = products[side][start : start + half]
                        at = slice(shift * part + side * half, shift * part + (side + 1) * half)
                        if tap == 0 or (tap == 1 and plane == 0):
                            acc_ref[target, at] = piece
                        else:
                            acc_ref[target, at] += piece

    column = lax.broadcasted_iota(jnp.int32, (part, n_cols), 1)
    row = lax.broadcasted_iota(jnp.int32, (part, n_cols), 0)
    hidden = (row < part // (2 * half_r + 2)) & (first_strip_ref[0] == 1)
    cost_ref[0] = jnp.zeros(cost_ref.shape[1:], cost_ref.dtype)

    def finish(plane):
        left = jnp.where(column == 0, 0.0, pltpu.roll(acc_ref[plane, 0:part], 1, 1))
        right = jnp.where(
            column == n_cols - 1, 0.0, pltpu.roll(acc_ref[plane, 2 * part : 3 * part], n_cols - 1, 1)
        )
        total = acc_ref[plane, part : 2 * part] + left + right + b1_ref[...]
        cost = jnp.where(hidden, 0.0, jnp.maximum(total, 0.0)).astype(jnp.bfloat16)
        spread = jnp.dot(cost, pick_ref[...], preferred_element_type=jnp.float32)
        spread = spread.astype(jnp.bfloat16)
        for tap in range(3):
            cost_ref[plane + 1, tap * part : (tap + 1) * part] = spread[
                :, tap * wide : (tap + 1) * wide
            ]

    def second(q):
        block = cost_ref[2 * q : 2 * q + 3].reshape(9 * part, wide)
        result = jnp.dot(w2_ref[...], block, preferred_element_type=jnp.float32)
        result = result + b2_ref[...]
        out_ref[q] = result[:, :half_x].reshape(half_r, c2, half_x)

    for plane in range(planes):
        one_plane(plane)
        if plane >= 1:
            finish(plane - 1)
            if plane % 2 == 0:
                second(plane // 2 - 1)
    finish(planes - 1)
    second(half_p - 1)


def prepare(conv_first, rows_n, n_cols, wide):
    taps_p, taps_r, c1, taps_x, channels = conv_first.shape
    half_rows = (rows_n + 2) // 2
    width = (half_rows + 2) * channels
    lanes = -(-width // 128) * 128
    groups = taps_p * taps_x
    moved = jnp.transpose(conv_first, (0, 3, 2, 1, 4)).reshape(groups, c1, taps_r * channels)
    moved = jnp.pad(moved, ((0, 0), (0, 0), (0, lanes - taps_r * channels)))
    vmem = pl.BlockSpec(memory_space=pltpu.VMEM)
    return pl.pallas_call(
        prepare_kernel,
        out_shape=[
            jax.ShapeDtypeStruct((groups * half_rows * c1, width), jnp.bfloat16),
            jax.ShapeDtypeStruct((n_cols, 3 * wide), jnp.bfloat16),
        ],
        in_specs=[vmem],
        out_specs=[vmem] * 2,
        cost_estimate=pl.CostEstimate(flops=2000000, bytes_accessed=1200000, transcendentals=0),
        compiler_params=pltpu.CompilerParams(vmem_limit_bytes=8 << 20),
        name="prepare",
    )(moved)


def banded_second(conv_second, rows_n):
    c2, taps_p, taps_r, taps_x, c1 = conv_second.shape
    moved = jnp.transpose(conv_second, (0, 1, 3, 2, 4))
    bands = [
        jnp.pad(
            moved, ((0, 0), (0, 0), (0, 0), (2 * g, rows_n + 2 - taps_r - 2 * g), (0, 0))
        ).reshape(c2, -1)
        for g in range(rows_n // 2)
    ]
    return jnp.concatenate(bands, axis=0)


def on_device(
    ref_features,
    source_tiles,
    pair_lists,
    view_counts,
    disparities,
    conv_first,
    bias_first,
    conv_second,
    bias_second,
):
    n_view = lax.axis_size("view")
    rows_n, channels, n_cols = ref_features.shape
    tiles_dev = source_tiles.shape[0]
    _, sources, blocks = pair_lists.shape
    planes = disparities.shape[0]
    c1 = conv_first.shape[2]
    c2 = conv_second.shape[0]
    request_total = sources * blocks
    slot_cap = max(2, (request_total + n_view - 1) // n_view)
    flat_ids = pair_lists.reshape(request_total)
    slot_ids, local_ids = request_slots(flat_ids, slot_cap, tiles_dev)
    wanted = request_table(slot_ids, local_ids, n_view, slot_cap)
    asked = ask_owners(wanted)
    outgoing = source_tiles[jnp.maximum(asked, 0)]
    arrived = lax.all_to_all(outgoing, "view", split_axis=0, concat_axis=0, tiled=True)
    arrived = arrived.reshape(n_view * slot_cap, 2 * channels, n_cols)
    w2 = banded_second(conv_second, rows_n)
    part = (rows_n + 2) * c1
    half_x = n_cols // 2
    wide = -(-half_x // 128) * 128
    b1 = jnp.broadcast_to(bias_first[None, :, None], (rows_n + 2, c1, 1)).reshape(part, 1)
    b2 = jnp.broadcast_to(bias_second[None, :, None], (rows_n // 2, c2, 1)).reshape(-1, 1)
    w1, pick = prepare(conv_first, rows_n, n_cols, wide)
    ready = (arrived, w1, w2, b1, b2, pick)
    arrived, w1, w2, b1, b2, pick = lax.optimization_barrier(ready)
    slots = slot_ids.reshape(sources, blocks)
    ref_flat = ref_features.reshape(rows_n * channels, n_cols)
    warp = functools.partial(variance, slots=slots, disparities=disparities)
    warp = functools.partial(warp, view_counts=view_counts, arrived=arrived, ref_flat=ref_flat)
    low, top = warp(((rows_n - 2, rows_n - 1), (0,)))
    above = passed_along(low, "view", 1)
    below = passed_along(top, "view", -1)
    (mid,) = warp((tuple(range(1, rows_n - 2)),))
    smem = pl.BlockSpec(memory_space=pltpu.SMEM)
    vmem = pl.BlockSpec(memory_space=pltpu.VMEM)
    first_strip = (lax.axis_index("view") == 0).astype(jnp.int32).reshape(1)
    return pl.pallas_call(
        conv_kernel,
        out_shape=jax.ShapeDtypeStruct((planes // 2, rows_n // 2, c2, half_x), jnp.float32),
        in_specs=[smem] + [vmem] * 10,
        out_specs=vmem,
        scratch_shapes=[
            pltpu.VMEM((planes, 3 * part, n_cols), jnp.float32),
            pltpu.VMEM((planes + 1, 3 * part, wide), jnp.bfloat16),
        ],
        compiler_params=pltpu.CompilerParams(vmem_limit_bytes=24 << 20),
        name="convolutions",
    )(first_strip, above, top, mid, low, below, w1, b1, w2, b2, pick)


def solution(mesh):
    return jax.shard_map(
        on_device,
        mesh=mesh,
        in_specs=(
            P(("groups", "view"), None, None),
            P(("groups", "view"), None, None, None),
            P(("groups", "view"), None, None),
            P(("groups", "view")),
            P("groups", None),
            P(),
            P(),
            P(),
            P(),
        ),
        out_specs=P("groups", "view", None, None),
        check_vma=False,
    )
```
